32 devices in a mesh: groups: 2 (over y), seq: 4 (over z), dp: 4 (over x, core).
Axes of the slice: x: 2, y: 2, z: 4, core: 2. Of those that a mesh axis runs over, the one named last changes fastest.
Arguments:
- inputs: bfloat16 [8, 4096, 448], P(('groups', 'dp'), 'seq'), parts along dimension 0, may hold values from -6 to 6
- cotangent: bfloat16 [8, 4096, 448], P(('groups', 'dp'), 'seq'), parts along dimension 0, may hold values from -6 to 6
- first_weight_matrix: bfloat16 [3, 448, 448], P(None, None, 'dp'), may hold values from -0.15625 to 0.15625
- weight_two: bfloat16 [3, 448, 448], P(None, None, 'dp'), may hold values from -0.15625 to 0.15625
Outputs:
- input_grad: bfloat16 [8, 4096, 448], P(('groups', 'dp'), 'seq'), parts along dimension 0
- grad_one: float32 [6, 448, 448], P('groups', None, 'dp'), parts along dimension 0
- grad_two: float32 [6, 448, 448], P('groups', None, 'dp'), parts along dimension 0
The draws below stay inside these ranges and needn't reach their ends.
There are 2 independent parts, one for each index of `groups`. The reference program is written for one: setup_inputs(seed, part) draws one part's arguments, and reference() takes and returns one part's arrays. A program takes and returns all parts, laid end to end along the dimension named above; an argument that names none is the same for every part. Nothing has to cross between parts.
All inputs are finite; a program needn't handle non-finite values.
Results may differ from the reference program's by a relative error of at most 0.012.
Values may be sent and summed in bfloat16 or wider, within the bound.
No kernel may reach another device: no remote copies, remote signals or barrier semaphores. Data moves between devices by JAX's collectives and lax.ppermute only.
A program may use at most 64 MiB of HBM per device.

```python
import math
import jax
import jax.numpy as jnp
from jax import lax

C = 448
POS_DEV = 1024
SEQS = 4
LEN = 4096
FIRST_SPACING = 2048
SECOND_SPACING = 4096
N_SEQ = 4


def spiked(drawn, own_key, source, target, parts, factor):
    owner, partner = [(jnp.arange(drawn.shape[axis_at]) // (drawn.shape[axis_at] // parts)).reshape([-1 if axis == axis_at else 1 for axis in range(drawn.ndim)]) for axis_at in (source, target)]
    chosen = jax.random.permutation(own_key, parts)[partner]
    strong = (owner == chosen) | (owner == (partner + parts // 2) % parts)
    return jnp.where(strong, factor * drawn, drawn)


def level_of(stream_key, shape, cuts, low, top_value):
    gain = 1.0
    for axis_at, parts in cuts:
        draws = jax.random.uniform(jax.random.fold_in(jax.random.fold_in(stream_key, 6), axis_at), (parts,), jnp.float32, low / len(cuts), top_value / len(cuts))
        gain = gain * jnp.repeat(jnp.exp(draws), shape[axis_at] // parts).reshape((-1,) + (1,) * (len(shape) - 1 - axis_at))
    return gain


def normal_values(own_key, dims, scale, bound, split=(), held_as=jnp.bfloat16):
    array = scale * jax.random.normal(own_key, dims, jnp.float32)
    if split:
        array = array * level_of(own_key, dims, split, -0.22, 0.18)
    return jnp.clip(array, -bound, bound).astype(held_as)


def bell_draw_with(rng, shape, spread, limit, cuts, heavy, held_as=jnp.bfloat16):
    drawn = spread * jax.random.normal(rng, shape, jnp.float32)
    if cuts:
        drawn = drawn * level_of(rng, shape, cuts, -0.22, 0.18)
    return jnp.clip(spiked(drawn, jax.random.fold_in(rng, 3), *heavy), -limit, limit).astype(held_as)


def setup_inputs(seed: int = 0, part: int = 0) -> dict:
    key_of = jax.random.split(jax.random.key(seed), 5)
    part_keys = jax.random.split(jax.random.fold_in(key_of[4], part), 5)
    return {
        "inputs": normal_values(part_keys[0], (SEQS, LEN, C), 1.0, 6.0, ((0, 4), (1, 4))),
        "cotangent": bell_draw_with(part_keys[1], (SEQS, LEN, C), 1.0, 6.0, ((0, 4), (1, 4)), (0, 2, 4, 2.0)),
        "first_weight_matrix": normal_values(key_of[2], (3, C, C), (3 * C) ** -0.5, 0.15625, ((2, 4),)),
        "weight_two": normal_values(key_of[3], (3, C, C), (3 * C) ** -0.5, 0.15625, ((2, 4),)),
    }


def gelu_slope(value):
    return jax.vjp(jax.nn.gelu, value)[1](jnp.ones_like(value))[0]

def displaced_rows(values, offset):
    count = values.shape[0]
    if offset >= count or -offset >= count:
        return jnp.zeros_like(values)
    filler = jnp.zeros((abs(offset), values.shape[1]), values.dtype)
    if offset > 0:
        return jnp.concatenate([filler, values[:count - offset]], axis=0)
    return jnp.concatenate([values[-offset:], filler], axis=0)

def block_terms(left, right, factor):
    left_blocks = left.reshape(N_SEQ, POS_DEV, C).astype(jnp.float32)
    right_blocks = right.reshape(N_SEQ, POS_DEV, C).astype(jnp.float32)
    terms = jnp.einsum('bpc,bpd->bcd', left_blocks, right_blocks) * factor
    rounded = lax.optimization_barrier(terms.astype(jnp.bfloat16))
    return lax.optimization_barrier(jnp.sum(rounded.astype(jnp.float32), axis=0))

def one_sequence(inputs, cotangent, first_weight_matrix, weight_two, factor):
    input_activation = jax.nn.gelu(inputs.astype(jnp.float32)).astype(jnp.bfloat16)
    preactivation = jnp.dot(displaced_rows(input_activation, FIRST_SPACING), first_weight_matrix[0], preferred_element_type=jnp.float32)
    preactivation = preactivation + jnp.dot(input_activation, first_weight_matrix[1], preferred_element_type=jnp.float32)
    preactivation = preactivation + jnp.dot(displaced_rows(input_activation, -FIRST_SPACING), first_weight_matrix[2], preferred_element_type=jnp.float32)
    hidden_f = (inputs.astype(jnp.float32) + preactivation).astype(jnp.bfloat16).astype(jnp.float32)
    act_one = jax.nn.gelu(hidden_f).astype(jnp.bfloat16)
    second_layer_taps = [displaced_rows(cotangent, -SECOND_SPACING), cotangent, displaced_rows(cotangent, SECOND_SPACING)]
    delta_one = jnp.zeros(inputs.shape, jnp.float32)
    for k in range(3):
        delta_one = delta_one + jnp.dot(second_layer_taps[k], weight_two[k].T, preferred_element_type=jnp.float32)
    middle_gradient = (cotangent.astype(jnp.float32) + gelu_slope(hidden_f) * delta_one).astype(jnp.bfloat16)
    first_layer_taps = [displaced_rows(middle_gradient, -FIRST_SPACING), middle_gradient, displaced_rows(middle_gradient, FIRST_SPACING)]
    delta_zero = jnp.zeros(inputs.shape, jnp.float32)
    for k in range(3):
        delta_zero = delta_zero + jnp.dot(first_layer_taps[k], first_weight_matrix[k].T, preferred_element_type=jnp.float32)
    inputs_f = inputs.astype(jnp.float32)
    input_grad = (middle_gradient.astype(jnp.float32) + gelu_slope(inputs_f) * delta_zero).astype(jnp.bfloat16)
    grad_two = jnp.stack([block_terms(act_one, second_layer_taps[k], factor) for k in range(3)])
    grad_one = jnp.stack([block_terms(input_activation, first_layer_taps[k], factor) for k in range(3)])
    return (input_grad, grad_one, grad_two)

def reference(inputs, cotangent, first_weight_matrix, weight_two):
    factor = 1.0 / math.sqrt(SEQS * LEN)

    def run(pair):
        return one_sequence(pair[0], pair[1], first_weight_matrix, weight_two, factor)
    input_grad, grad_one, grad_two = lax.map(run, (inputs, cotangent))
    return (input_grad, lax.optimization_barrier(jnp.sum(grad_one, axis=0)), lax.optimization_barrier(jnp.sum(grad_two, axis=0)))
```

```python
import functools
import math

import jax
import jax.numpy as jnp
from jax import lax
from jax.experimental import pallas as pl
from jax.experimental.pallas import tpu as pltpu
from jax.sharding import PartitionSpec as P

FIRST_SHIFT = 2
SECOND_SHIFT = 4
CHUNKS = (2, 2)
F32 = jnp.float32
BF16 = jnp.bfloat16


def gelu_pair(x):
    s = math.sqrt(2.0 / math.pi)
    square = x * x
    half = 0.5 + 0.5 * jnp.tanh(x * (s + (0.044715 * s) * square))
    bend = x * (2.0 * s + (6.0 * 0.044715 * s) * square)
    return x * half, half * (1.0 + (1.0 - half) * bend)


def dot_nn(a, b):
    return lax.dot_general(a, b, (((1,), (0,)), ((), ())), preferred_element_type=F32)


def dot_nt(a, b):
    return lax.dot_general(a, b, (((1,), (1,)), ((), ())), preferred_element_type=F32)


def dot_tn(a, b):
    return lax.dot_general(a, b, (((0,), (0,)), ((), ())), preferred_element_type=F32)


VMEM = pl.BlockSpec(memory_space=pltpu.VMEM)
SMEM = pl.BlockSpec(memory_space=pltpu.SMEM)
ANY = pl.BlockSpec(memory_space=pl.ANY)
HBM = pl.BlockSpec(memory_space=pltpu.HBM)


def call(body, name, out, operands, specs, out_specs=None, scratch=(), aliases=None, limit=8):
    return pl.pallas_call(
        body,
        out_shape=[jax.ShapeDtypeStruct(*o) for o in out],
        in_specs=specs,
        out_specs=out_specs or [VMEM] * len(out),
        scratch_shapes=scratch,
        input_output_aliases=aliases or {},
        compiler_params=pltpu.CompilerParams(vmem_limit_bytes=limit << 20),
        name=name,
    )(*operands)


def lanes(start, size):
    return pl.ds(pl.multiple_of(start, 128), size)


def pack_kernel(where, x_ref, c_ref, *refs):
    wires, sems = refs[:-1], refs[-1]
    copies, start = [], 0
    for c, wire in enumerate(wires):
        size = wire.shape[2]
        for j, ref in enumerate((x_ref, c_ref)):
            source = ref.at[:, lanes(where[4] + start, size)]
            copies.append(pltpu.make_async_copy(source, wire.at[j], sems.at[2 * c + j]))
        start += size
    for copy in copies:
        copy.start()
    for copy in copies:
        copy.wait()


def turn_kernel(w_ref, w2_ref, after_ref, out_ref, taps, sems):
    del after_ref
    copies = [
        pltpu.make_async_copy(w_ref, taps.at[pl.ds(0, 3)], sems.at[0]),
        pltpu.make_async_copy(w2_ref.at[1], taps.at[3], sems.at[1]),
    ]
    for copy in copies:
        copy.start()
    for copy in copies:
        copy.wait()
    for k in range(4):
        out_ref[k] = taps[k].T


def join_kernel(where, *refs):
    pieces, (out_ref, across_ref) = refs[:-2], refs[-2:]
    shard = pieces[0].shape[1]
    for m, ref in enumerate(pieces):
        rows = pl.ds(pl.multiple_of(lax.bitwise_xor(where[3], m) * shard, 16), shard)
        for k in range(4):
            out_ref[k, rows, :] = ref[k]
    for k in range(4):
        across_ref[k] = out_ref[k].T


def both(o_ref, where, start, size, wire):
    return jnp.concatenate([o_ref[:, lanes(where[0] + start, size)], wire], axis=1)


def ahead_kernel(start, first, last, factor, where, x_ref, c_ref, wire_ref, w_ref, across_ref, *refs):
    if not first:
        sums_in, refs = refs[0], refs[1:]
    mid_ref, refs = refs[0], refs[1:]
    size = wire_ref.shape[2]
    q = where[1]
    r = 2 - q
    x = both(x_ref, where, start, size, wire_ref[0]).astype(F32)
    cot = both(c_ref, where, start, size, wire_ref[1])
    act = gelu_pair(x)[0].astype(BF16)
    act_o, act_p = act[:, :size], act[:, size:]
    cross = jnp.concatenate([dot_nn(w_ref[q], act_p), dot_nn(w_ref[r], act_o)], axis=1)
    hidden = (x + dot_nn(w_ref[1], act) + cross).astype(BF16).astype(F32)
    act_one, slope_one = gelu_pair(hidden)
    mid = (cot.astype(F32) + slope_one * dot_nn(across_ref[3], cot)).astype(BF16)
    mid_ref[...] = mid
    mid_o, mid_p = mid[:, :size], mid[:, size:]
    terms = (
        (3, cot, act_one.astype(BF16)),
        (1, mid, act),
        (q, mid_o, act_p),
        (r, mid_p, act_o),
    )
    if not last:
        (sums,) = refs
        for k, left, right in terms:
            value = dot_nt(left, right)
            sums[k] = value if first else sums_in[k] + value
        return
    keep_ref, give_ref, total = refs
    for k, left, right in terms:
        total[k] = ((sums_in[k] + dot_nt(left, right)) * factor).astype(BF16)
    shard = keep_ref.shape[2]
    for ref, core in ((keep_ref, where[2]), (give_ref, 1 - where[2])):
        for j in range(2):
            side = lax.bitwise_xor(where[6], 1 - j)
            rows = pl.ds(pl.multiple_of((2 * side + core) * shard, 16), shard)
            for k in range(2):
                level = lax.bitwise_xor(where[5], 1 - k)
                pair = [total[level, rows, :], total[level + 2, rows, :]]
                ref[j, k] = jnp.concatenate(pair, axis=1)


def back_kernel(start, where, x_ref, wire_ref, mid_ref, across_ref, own_ref, give_ref):
    size = wire_ref.shape[2]
    q = where[1]
    r = 2 - q
    slope = gelu_pair(both(x_ref, where, start, size, wire_ref[0]).astype(F32))[1]
    mid = mid_ref[...]
    mid_o, mid_p = mid[:, :size], mid[:, size:]
    cross = jnp.concatenate([dot_nn(across_ref[r], mid_p), dot_nn(across_ref[q], mid_o)], axis=1)
    delta = dot_nn(across_ref[1], mid) + cross
    grad = (mid.astype(F32) + slope * delta).astype(BF16)
    own_ref[...] = grad[:, :size]
    give_ref[...] = grad[:, size:]


def finish_kernel(where, mine_ref, theirs_ref, one_ref, two_ref):
    chans = one_ref.shape[1]
    even = where[5] == 0
    mine, theirs = mine_ref[...], theirs_ref[...]
    for want, taps in ((even, ((one_ref, 0), (one_ref, 2))), (~even, ((one_ref, 1), (two_ref, 1)))):
        terms = jnp.where(want, mine, theirs).astype(F32)
        for j, (out, k) in enumerate(taps):
            out[k] = terms[:, j * chans : (j + 1) * chans].T
    two_ref[0] = jnp.zeros(two_ref.shape[1:], F32)
    two_ref[2] = jnp.zeros(two_ref.shape[1:], F32)


def place_kernel(where, *refs):
    out_ref, refs = refs[-1], refs[:-2]
    count = len(CHUNKS)
    for base, pieces in ((where[0], refs[:count]), (where[4], refs[count:])):
        start = 0
        for ref in pieces:
            out_ref[:, lanes(base + start, ref.shape[1])] = ref[...]
            start += ref.shape[1]


def swapped(value, axis, bit):
    route = [(i, i ^ bit) for i in range(lax.axis_size(axis))]
    return lax.ppermute(value, axis, route)


def added(a, b):
    return (a.astype(F32) + b.astype(F32)).astype(BF16)


def on_pairs(inputs, cotangent, first_weight_matrix, weight_two):
    chans = inputs.shape[2]
    block = inputs.shape[1]
    shard = chans // 4
    half = block // 2
    sizes = [half * part // sum(CHUNKS) for part in CHUNKS]
    factor = 1.0 / math.sqrt(
        inputs.shape[0] * lax.axis_size("dp") * inputs.shape[1] * lax.axis_size("seq")
    )
    seq, dp = lax.axis_index("seq"), lax.axis_index("dp")
    low = seq < FIRST_SHIFT
    keep_at = jnp.where(low, 0, half)
    level, side, core = seq % 2, dp // 2, dp % 2
    where = jnp.stack([keep_at, jnp.where(low, 2, 0), core, dp, half - keep_at, level, side])
    where = where.astype(jnp.int32)
    x, cot = inputs.reshape(block, chans).T, cotangent.reshape(block, chans).T

    packed = call(
        pack_kernel,
        "pack",
        [((2, chans, size), BF16) for size in sizes],
        [where, x, cot],
        [SMEM, HBM, HBM],
        scratch=[pltpu.SemaphoreType.DMA((2 * len(sizes),))],
    )
    wires = [swapped(wire, "seq", FIRST_SHIFT) for wire in packed]
    (own_shard,) = call(
        turn_kernel,
        "turn",
        [((4, shard, chans), BF16)],
        [first_weight_matrix, weight_two, packed[-1]],
        [HBM, HBM, ANY],
        scratch=[pltpu.VMEM((4, chans, shard), BF16), pltpu.SemaphoreType.DMA((2,))],
    )
    shards = [own_shard] + [swapped(own_shard, "dp", m) for m in (1, 2, 3)]
    w, across = call(
        join_kernel,
        "join",
        [((4, chans, chans), BF16)] * 2,
        [where, *shards],
        [SMEM] + [VMEM] * 4,
    )

    start, sums, own, back = 0, [], [], []
    for c, size in enumerate(sizes):
        last = c == len(sizes) - 1
        out = [((chans, 2 * size), BF16)]
        out += [((2, 2, shard, 2 * chans), BF16)] * 2 if last else [((4, chans, chans), F32)]
        operands = [where, x, cot, wires[c], w, across] + sums
        mid, *rest = call(
            functools.partial(ahead_kernel, start, c == 0, last, factor),
            f"ahead_{c}",
            out,
            operands,
            [SMEM] + [VMEM] * (len(operands) - 1),
            scratch=[pltpu.VMEM((4, chans, chans), BF16)] if last else [],
            aliases={6: 1} if sums and not last else {},
        )
        if last:
            keep, give = rest
        else:
            sums = rest
        mine, theirs = call(
            functools.partial(back_kernel, start),
            f"back_{c}",
            [((chans, size), BF16)] * 2,
            [where, x, wires[c], mid, across],
            [SMEM] + [VMEM] * 4,
        )
        own.append(mine)
        back.append(theirs)
        start += size

    back[0], give = lax.optimization_barrier((back[0], give))
    whole = jnp.concatenate(back, axis=1)
    returned = [swapped(part, "seq", FIRST_SHIFT) for part in (whole[:, :128], whole[:, 128:])]
    got_core = swapped(give, "dp", 1)
    theirs = swapped(added(keep[0], got_core[0]), "dp", 2)
    mine = added(keep[1], got_core[1])
    theirs, returned[0] = lax.optimization_barrier((theirs, returned[0]))
    theirs, mine = added(mine[0], theirs[0]), added(mine[1], theirs[1])
    theirs, returned[1] = lax.optimization_barrier((swapped(theirs, "seq", 1), returned[1]))
    mine = added(mine, theirs)
    mine = added(mine, swapped(mine, "seq", 2))
    theirs = swapped(mine, "seq", 1)
    (input_grad,) = call(
        place_kernel,
        "place",
        [((chans, block), BF16)],
        [where, *own, *returned, mine],
        [SMEM] + [VMEM] * (len(own) + len(returned)) + [ANY],
    )
    grad_one, grad_two = call(
        finish_kernel,
        "finish",
        [((3, chans, shard), F32)] * 2,
        [where, mine, theirs],
        [SMEM, VMEM, VMEM],
    )
    return (input_grad.T.reshape(inputs.shape), grad_one, grad_two)


def shifted(block, axis, distance):
    devices = range(lax.axis_size(axis))
    route = [(i - distance, i) for i in devices if i - distance in devices]
    return lax.ppermute(block, axis, route)


def gelu_slope(value):
    return jax.vjp(jax.nn.gelu, value)[1](jnp.ones_like(value))[0]


def outer_terms(left, right, factor):
    product = lax.dot_general(
        left, right, (((0,), (0,)), ((), ())), preferred_element_type=jnp.float32
    )
    return product * factor


def back_product(tap, weight):
    return lax.dot_general(
        tap, weight, (((1,), (1,)), ((), ())), preferred_element_type=jnp.float32
    )


def on_shifts(inputs, cotangent, first_weight_matrix, weight_two):
    chans = inputs.shape[2]
    rows = inputs.shape[0] * inputs.shape[1]
    factor = 1.0 / math.sqrt(
        inputs.shape[0] * lax.axis_size("dp") * inputs.shape[1] * lax.axis_size("seq")
    )
    full_one = lax.all_gather(first_weight_matrix, "dp", axis=2, tiled=True)
    flat_in = inputs.reshape(rows, chans)
    inputs_f = flat_in.astype(jnp.float32)
    input_activation = jax.nn.gelu(inputs_f).astype(jnp.bfloat16)
    act_before = shifted(input_activation, "seq", 2)
    act_after = shifted(input_activation, "seq", -2)
    flat_cot = cotangent.reshape(rows, chans)
    cot_later = shifted(flat_cot, "seq", -4)
    cot_earlier = shifted(flat_cot, "seq", 4)
    preactivation = jnp.dot(act_before, full_one[0], preferred_element_type=jnp.float32)
    preactivation = preactivation + jnp.dot(
        input_activation, full_one[1], preferred_element_type=jnp.float32
    )
    preactivation = preactivation + jnp.dot(
        act_after, full_one[2], preferred_element_type=jnp.float32
    )
    hidden_f = (inputs_f + preactivation).astype(jnp.bfloat16).astype(jnp.float32)
    act_one = jax.nn.gelu(hidden_f).astype(jnp.bfloat16)
    full_two = lax.all_gather(weight_two, "dp", axis=2, tiled=True)
    second_layer_taps = (cot_later, flat_cot, cot_earlier)
    delta_one = back_product(second_layer_taps[0], full_two[0])
    delta_one = delta_one + back_product(second_layer_taps[1], full_two[1])
    delta_one = delta_one + back_product(second_layer_taps[2], full_two[2])
    middle_gradient = (flat_cot.astype(jnp.float32) + gelu_slope(hidden_f) * delta_one).astype(
        jnp.bfloat16
    )
    part_two = jnp.stack(
        [outer_terms(act_one, second_layer_taps[k], factor) for k in range(3)]
    ).astype(jnp.bfloat16)
    grad_two = lax.psum(
        lax.psum_scatter(part_two, "dp", scatter_dimension=2, tiled=True).astype(jnp.float32), "seq"
    )
    grad_later = shifted(middle_gradient, "seq", -2)
    grad_earlier = shifted(middle_gradient, "seq", 2)
    first_layer_taps = (grad_later, middle_gradient, grad_earlier)
    delta_zero = back_product(first_layer_taps[0], full_one[0])
    delta_zero = delta_zero + back_product(first_layer_taps[1], full_one[1])
    delta_zero = delta_zero + back_product(first_layer_taps[2], full_one[2])
    input_grad = (middle_gradient.astype(jnp.float32) + gelu_slope(inputs_f) * delta_zero).astype(
        jnp.bfloat16
    )
    part_one = jnp.stack(
        [outer_terms(input_activation, first_layer_taps[k], factor) for k in range(3)]
    ).astype(jnp.bfloat16)
    grad_one = lax.psum(
        lax.psum_scatter(part_one, "dp", scatter_dimension=2, tiled=True).astype(jnp.float32), "seq"
    )
    return (input_grad.reshape(inputs.shape), grad_one, grad_two)


def on_device(inputs, *others):
    seq, dp = lax.axis_size("seq"), lax.axis_size("dp")
    if (
        seq == 2 * FIRST_SHIFT
        and seq <= SECOND_SHIFT
        and dp == 4
        and inputs.shape[0] == 1
        and inputs.shape[1] % (256 * sum(CHUNKS)) == 0
    ):
        return on_pairs(inputs, *others)
    return on_shifts(inputs, *others)


def solution(mesh):
    placed = (
        P(("groups", "dp"), "seq", None),
        P(("groups", "dp"), "seq", None),
        P(None, None, "dp"),
        P(None, None, "dp"),
    )
    return jax.shard_map(
        on_device,
        mesh=mesh,
        in_specs=placed,
        out_specs=(
            P(("groups", "dp"), "seq", None),
            P("groups", None, "dp"),
            P("groups", None, "dp"),
        ),
        check_vma=False,
    )
```

```python
import functools
import math

import jax
import jax.numpy as jnp
from jax import lax
from jax.experimental import pallas as pl
from jax.experimental.pallas import tpu as pltpu
from jax.sharding import PartitionSpec as P

FIRST_SHIFT = 2
SECOND_SHIFT = 4
CHUNKS = 2
F32 = jnp.float32
BF16 = jnp.bfloat16


def gelu_pair(x):
    s = math.sqrt(2.0 / math.pi)
    square = x * x
    half = 0.5 + 0.5 * jnp.tanh(x * (s + (0.044715 * s) * square))
    bend = x * (2.0 * s + (6.0 * 0.044715 * s) * square)
    return x * half, half * (1.0 + (1.0 - half) * bend)


def dot_nn(a, b):
    return lax.dot_general(a, b, (((1,), (0,)), ((), ())), preferred_element_type=F32)


def dot_nt(a, b):
    return lax.dot_general(a, b, (((1,), (1,)), ((), ())), preferred_element_type=F32)


def dot_tn(a, b):
    return lax.dot_general(a, b, (((0,), (0,)), ((), ())), preferred_element_type=F32)


VMEM = pl.BlockSpec(memory_space=pltpu.VMEM)
SMEM = pl.BlockSpec(memory_space=pltpu.SMEM)
ANY = pl.BlockSpec(memory_space=pl.ANY)
HBM = pl.BlockSpec(memory_space=pltpu.HBM)


def call(body, name, out, operands, specs, out_specs=None, scratch=(), aliases=None, limit=8):
    return pl.pallas_call(
        body,
        out_shape=[jax.ShapeDtypeStruct(*o) for o in out],
        in_specs=specs,
        out_specs=out_specs or [VMEM] * len(out),
        scratch_shapes=scratch,
        input_output_aliases=aliases or {},
        compiler_params=pltpu.CompilerParams(vmem_limit_bytes=limit << 20),
        name=name,
    )(*operands)


def lanes(start, size):
    return pl.ds(pl.multiple_of(start, 128), size)


def pack_kernel(start, where, x_ref, c_ref, *refs):
    wire_ref, sems = refs[-2:]
    at = lanes(where[4] + start, wire_ref.shape[2])
    copies = [
        pltpu.make_async_copy(ref.at[:, at], wire_ref.at[j], sems.at[j])
        for j, ref in enumerate((x_ref, c_ref))
    ]
    for copy in copies:
        copy.start()
    for copy in copies:
        copy.wait()


def turn_kernel(w_ref, w2_ref, after_ref, out_ref, taps, sems):
    del after_ref
    copies = [
        pltpu.make_async_copy(w_ref, taps.at[pl.ds(0, 3)], sems.at[0]),
        pltpu.make_async_copy(w2_ref.at[1], taps.at[3], sems.at[1]),
    ]
    for copy in copies:
        copy.start()
    for copy in copies:
        copy.wait()
    for k in range(4):
        out_ref[k] = taps[k].T


def join_kernel(where, *refs):
    pieces, (out_ref, across_ref) = refs[:-2], refs[-2:]
    shard = pieces[0].shape[1]
    for m, ref in enumerate(pieces):
        rows = pl.ds(pl.multiple_of(lax.bitwise_xor(where[3], m) * shard, 16), shard)
        for k in range(4):
            out_ref[k, rows, :] = ref[k]
    for k in range(4):
        across_ref[k] = out_ref[k].T


def both(o_ref, where, start, size, wire):
    return jnp.concatenate([o_ref[:, lanes(where[0] + start, size)], wire], axis=1)


def own_part(where, start, size, x_ref, c_ref, w_ref, across_ref, outs):
    act_ref, base_ref, cross_ref, delta_ref = outs
    at = lanes(where[0] + start, size)
    x = x_ref[:, at].astype(F32)
    act = gelu_pair(x)[0].astype(BF16)
    act_ref[...] = act
    base_ref[...] = x + dot_nn(w_ref[1], act)
    cross_ref[...] = dot_nn(w_ref[2 - where[1]], act)
    delta_ref[...] = dot_nn(across_ref[3], c_ref[:, at])


def weight_terms(q, cot, act, act_one, mid, size):
    act_o, act_p = act[:, :size], act[:, size:]
    mid_o, mid_p = mid[:, :size], mid[:, size:]
    return ((3, cot, act_one), (1, mid, act), (q, mid_o, act_p), (2 - q, mid_p, act_o))


def first_kernel(later, where, x_ref, c_ref, wire_ref, w_ref, across_ref, mid_ref, sums, *outs):
    size = wire_ref.shape[2]
    q = where[1]
    x = both(x_ref, where, 0, size, wire_ref[0]).astype(F32)
    cot = both(c_ref, where, 0, size, wire_ref[1])
    act = gelu_pair(x)[0].astype(BF16)
    act_o, act_p = act[:, :size], act[:, size:]
    cross = jnp.concatenate([dot_nn(w_ref[q], act_p), dot_nn(w_ref[2 - q], act_o)], axis=1)
    hidden = (x + dot_nn(w_ref[1], act) + cross).astype(BF16).astype(F32)
    act_one, slope_one = gelu_pair(hidden)
    mid = (cot.astype(F32) + slope_one * dot_nn(across_ref[3], cot)).astype(BF16)
    mid_ref[...] = mid
    for k, left, right in weight_terms(q, cot, act, act_one.astype(BF16), mid, size):
        sums[k] = dot_nt(left, right)
    own_part(where, size, later, x_ref, c_ref, w_ref, across_ref, outs)


def last_kernel(start, factor, where, c_ref, wire_ref, w_ref, across_ref, sums, *refs):
    act_ref, base_ref, cross_ref, delta_ref, mid_ref = refs[:5]
    outs, total = refs[5:-1], refs[-1]
    size = wire_ref.shape[2]
    q = where[1]
    x_p = wire_ref[0].astype(F32)
    cot_p = wire_ref[1]
    act_p = gelu_pair(x_p)[0].astype(BF16)
    hidden = jnp.concatenate(
        [
            base_ref[...] + dot_nn(w_ref[q], act_p),
            x_p + dot_nn(w_ref[1], act_p) + cross_ref[...],
        ],
        axis=1,
    )
    act_one, slope_one = gelu_pair(hidden.astype(BF16).astype(F32))
    cot = both(c_ref, where, start, size, cot_p)
    delta = jnp.concatenate([delta_ref[...], dot_nn(across_ref[3], cot_p)], axis=1)
    mid = (cot.astype(F32) + slope_one * delta).astype(BF16)
    mid_ref[...] = mid
    act = jnp.concatenate([act_ref[...], act_p], axis=1)
    for k, left, right in weight_terms(q, cot, act, act_one.astype(BF16), mid, size):
        total[k] = ((sums[k] + dot_nt(left, right)) * factor).astype(BF16)
    parts = [ref.shape[2] for ref in outs[::2]]
    shard = sum(parts)
    for given in range(2):
        core = lax.bitwise_xor(where[2], given)
        for j in range(2):
            side = lax.bitwise_xor(where[6], 1 - j)
            rows = pl.ds(pl.multiple_of((2 * side + core) * shard, 16), shard)
            for k in range(2):
                level = lax.bitwise_xor(where[5], 1 - k)
                pair = [total[level, rows, :], total[level + 2, rows, :]]
                pair = jnp.concatenate(pair, axis=1)
                first = 0
                for h, part in enumerate(parts):
                    outs[2 * h + given][j, k] = pair[first : first + part]
                    first += part


def back_kernel(start, where, x_ref, wire_ref, mid_ref, across_ref, own_ref, give_ref):
    size = wire_ref.shape[2]
    q = where[1]
    r = 2 - q
    slope = gelu_pair(both(x_ref, where, start, size, wire_ref[0]).astype(F32))[1]
    mid = mid_ref[...]
    mid_o, mid_p = mid[:, :size], mid[:, size:]
    cross = jnp.concatenate([dot_nn(across_ref[r], mid_p), dot_nn(across_ref[q], mid_o)], axis=1)
    delta = dot_nn(across_ref[1], mid) + cross
    grad = (mid.astype(F32) + slope * delta).astype(BF16)
    own_ref[...] = grad[:, :size]
    give_ref[...] = grad[:, size:]


def finish_kernel(other, where, *refs):
    (one_ref, two_ref), (turned, zeros, sems) = refs[-5:-3], refs[-3:]
    terms = refs[: len(refs) - 5 - (2 if other else 0)]
    chans = turned.shape[1]
    if not other:
        zeros[...] = jnp.zeros(zeros.shape, F32)
        blank = [pltpu.make_async_copy(zeros, two_ref.at[k], sems.at[2 + k]) for k in (0, 2)]
        for copy in blank:
            copy.start()
    rows = jnp.concatenate([ref[...].astype(F32) for ref in terms], axis=0)
    for j in range(2):
        turned[j] = rows[:, j * chans : (j + 1) * chans].T
    parity = lax.bitwise_xor(where[5], 1) if other else where[5]
    for want, places in ((0, ((one_ref, 0), (one_ref, 2))), (1, ((one_ref, 1), (two_ref, 1)))):

        @pl.when(parity == want)
        def _():
            copies = [
                pltpu.make_async_copy(turned.at[j], ref.at[k], sems.at[j])
                for j, (ref, k) in enumerate(places)
            ]
            for copy in copies:
                copy.start()
            for copy in copies:
                copy.wait()

    if not other:
        for copy in blank:
            copy.wait()


def finished(where, terms, chans, shard, held=()):
    return call(
        functools.partial(finish_kernel, bool(held)),
        "finish",
        [((3, chans, shard), F32)] * 2,
        [where, *terms, *held],
        [SMEM] + [VMEM] * len(terms) + [HBM] * len(held),
        out_specs=[HBM, HBM],
        scratch=[
            pltpu.VMEM((2, chans, shard), F32),
            pltpu.VMEM((chans, shard), F32),
            pltpu.SemaphoreType.DMA((5,)),
        ],
        aliases={len(terms) + 1 + j: j for j in range(len(held))},
    )


def place_kernel(plan, where, *refs):
    pieces, (out_ref, sems) = refs[: len(plan)], refs[-2:]
    copies = [
        pltpu.make_async_copy(
            ref,
            out_ref.at[pl.ds(row, ref.shape[0]), lanes(where[base] + start, ref.shape[1])],
            sems.at[i],
        )
        for i, (ref, (base, row, start)) in enumerate(zip(pieces, plan))
    ]
    for copy in copies:
        copy.start()
    for copy in copies:
        copy.wait()


def placed(where, plan, pieces, shape, after):
    (out,) = call(
        functools.partial(place_kernel, plan),
        "place",
        [(shape, BF16)],
        [where, *pieces, after],
        [SMEM] + [VMEM] * len(pieces) + [ANY],
        out_specs=[HBM],
        scratch=[pltpu.SemaphoreType.DMA((len(pieces),))],
    )
    return out


def in_hbm(value):
    return pltpu.with_memory_space_constraint(value, pltpu.HBM)


def swapped(value, axis, bit):
    route = [(i, i ^ bit) for i in range(lax.axis_size(axis))]
    return lax.ppermute(value, axis, route)


def added(a, b):
    return (a.astype(F32) + b.astype(F32)).astype(BF16)


def on_pairs(inputs, cotangent, first_weight_matrix, weight_two):
    chans = inputs.shape[2]
    block = inputs.shape[1]
    shard = chans // 4
    half = block // 2
    sizes = [half // CHUNKS] * CHUNKS
    factor = 1.0 / math.sqrt(
        inputs.shape[0] * lax.axis_size("dp") * inputs.shape[1] * lax.axis_size("seq")
    )
    seq, dp = lax.axis_index("seq"), lax.axis_index("dp")
    low = seq < FIRST_SHIFT
    keep_at = jnp.where(low, 0, half)
    level, side, core = seq % 2, dp // 2, dp % 2
    where = jnp.stack([keep_at, jnp.where(low, 2, 0), core, dp, half - keep_at, level, side])
    where = where.astype(jnp.int32)
    x, cot = inputs.reshape(block, chans).T, cotangent.reshape(block, chans).T

    packed, start = [], 0
    for size in sizes:
        packed += call(
            functools.partial(pack_kernel, start),
            "pack",
            [((2, chans, size), BF16)],
            [where, in_hbm(x), in_hbm(cot)] + packed[-1:],
            [SMEM, HBM, HBM] + [ANY] * len(packed[-1:]),
            scratch=[pltpu.SemaphoreType.DMA((2,))],
        )
        start += size
    wires = [swapped(wire, "seq", FIRST_SHIFT) for wire in packed]
    (own_shard,) = call(
        turn_kernel,
        "turn",
        [((4, shard, chans), BF16)],
        [in_hbm(first_weight_matrix), in_hbm(weight_two), packed[-1]],
        [HBM, HBM, ANY],
        scratch=[pltpu.VMEM((4, chans, shard), BF16), pltpu.SemaphoreType.DMA((2,))],
    )
    shards = [own_shard] + [swapped(own_shard, "dp", m) for m in (1, 2, 3)]
    w, across = call(
        join_kernel,
        "join",
        [((4, chans, chans), BF16)] * 2,
        [where, *shards],
        [SMEM] + [VMEM] * 4,
    )

    def backward(c, mid):
        return call(
            functools.partial(back_kernel, c * size),
            f"back_{c}",
            [((chans, size), BF16)] * 2,
            [where, x, wires[c], mid, across],
            [SMEM] + [VMEM] * 4,
        )

    size = half // CHUNKS
    own = []
    mid, *held = call(
        functools.partial(first_kernel, size),
        "first",
        [((chans, 2 * size), BF16), ((4, chans, chans), F32), ((chans, size), BF16)]
        + [((chans, size), F32)] * 3,
        [where, x, cot, wires[0], w, across],
        [SMEM] + [VMEM] * 5,
    )
    mine, theirs = backward(0, mid)
    own.append(mine)
    back = [theirs]
    back[0], wires[1] = lax.optimization_barrier((back[0], wires[1]))
    mid, *halves = call(
        functools.partial(last_kernel, size, factor),
        "last",
        [((chans, 2 * size), BF16)]
        + [((2, 2, shard // 2, 2 * chans), BF16)] * 4,
        [where, cot, wires[1], w, across, *held],
        [SMEM] + [VMEM] * 9,
        scratch=[pltpu.VMEM((4, chans, chans), BF16)],
    )

    tie = lambda *values: list(lax.optimization_barrier(values))
    keep, give = halves[0::2], halves[1::2]
    returned = [swapped(back[0], "seq", FIRST_SHIFT)]
    got = [swapped(v, "dp", 1) for v in give]
    send = [added(k[0], v[0]) for k, v in zip(keep, got)]
    mine = [added(k[1], v[1]) for k, v in zip(keep, got)]
    send[0], mid = tie(send[0], mid)
    own_last, theirs = backward(1, mid)
    own.append(own_last)
    cut = chans // 2
    first, second = theirs[:cut], theirs[cut:]
    send = tie(*send)
    got = [swapped(v, "dp", 2) for v in send]
    got[1], first = tie(got[1], first)
    returned.append(swapped(first, "seq", FIRST_SHIFT))
    send = [added(m[0], v[0]) for m, v in zip(mine, got)]
    mine = [added(m[1], v[1]) for m, v in zip(mine, got)]
    send[0], mine[1] = tie(send[0], mine[1])
    got = [swapped(v, "seq", 1) for v in send]
    got[0], second = tie(got[0], second)
    returned.append(swapped(second, "seq", FIRST_SHIFT))
    mine = [added(m, v) for m, v in zip(mine, got)]
    mine = [added(m, swapped(m, "seq", 2)) for m in mine]
    theirs = [swapped(m, "seq", 1) for m in mine]
    input_grad = placed(
        where,
        ((0, 0, 0), (0, 0, size), (4, 0, 0), (4, 0, size), (4, cut, size)),
        own + returned,
        (chans, block),
        mine[1],
    )
    held = finished(where, mine, chans, shard)
    grad_one, grad_two = finished(where, theirs, chans, shard, held)
    return (input_grad.T.reshape(inputs.shape), grad_one, grad_two)


def shifted(block, axis, distance):
    devices = range(lax.axis_size(axis))
    route = [(i - distance, i) for i in devices if i - distance in devices]
    return lax.ppermute(block, axis, route)


def gelu_slope(value):
    return jax.vjp(jax.nn.gelu, value)[1](jnp.ones_like(value))[0]


def outer_terms(left, right, factor):
    product = lax.dot_general(
        left, right, (((0,), (0,)), ((), ())), preferred_element_type=jnp.float32
    )
    return product * factor


def back_product(tap, weight):
    return lax.dot_general(
        tap, weight, (((1,), (1,)), ((), ())), preferred_element_type=jnp.float32
    )


def on_shifts(inputs, cotangent, first_weight_matrix, weight_two):
    chans = inputs.shape[2]
    rows = inputs.shape[0] * inputs.shape[1]
    factor = 1.0 / math.sqrt(
        inputs.shape[0] * lax.axis_size("dp") * inputs.shape[1] * lax.axis_size("seq")
    )
    full_one = lax.all_gather(first_weight_matrix, "dp", axis=2, tiled=True)
    flat_in = inputs.reshape(rows, chans)
    inputs_f = flat_in.astype(jnp.float32)
    input_activation = jax.nn.gelu(inputs_f).astype(jnp.bfloat16)
    act_before = shifted(input_activation, "seq", 2)
    act_after = shifted(input_activation, "seq", -2)
    flat_cot = cotangent.reshape(rows, chans)
    cot_later = shifted(flat_cot, "seq", -4)
    cot_earlier = shifted(flat_cot, "seq", 4)
    preactivation = jnp.dot(act_before, full_one[0], preferred_element_type=jnp.float32)
    preactivation = preactivation + jnp.dot(
        input_activation, full_one[1], preferred_element_type=jnp.float32
    )
    preactivation = preactivation + jnp.dot(
        act_after, full_one[2], preferred_element_type=jnp.float32
    )
    hidden_f = (inputs_f + preactivation).astype(jnp.bfloat16).astype(jnp.float32)
    act_one = jax.nn.gelu(hidden_f).astype(jnp.bfloat16)
    full_two = lax.all_gather(weight_two, "dp", axis=2, tiled=True)
    second_layer_taps = (cot_later, flat_cot, cot_earlier)
    delta_one = back_product(second_layer_taps[0], full_two[0])
    delta_one = delta_one + back_product(second_layer_taps[1], full_two[1])
    delta_one = delta_one + back_product(second_layer_taps[2], full_two[2])
    middle_gradient = (flat_cot.astype(jnp.float32) + gelu_slope(hidden_f) * delta_one).astype(
        jnp.bfloat16
    )
    part_two = jnp.stack(
        [outer_terms(act_one, second_layer_taps[k], factor) for k in range(3)]
    ).astype(jnp.bfloat16)
    grad_two = lax.psum(
        lax.psum_scatter(part_two, "dp", scatter_dimension=2, tiled=True).astype(jnp.float32), "seq"
    )
    grad_later = shifted(middle_gradient, "seq", -2)
    grad_earlier = shifted(middle_gradient, "seq", 2)
    first_layer_taps = (grad_later, middle_gradient, grad_earlier)
    delta_zero = back_product(first_layer_taps[0], full_one[0])
    delta_zero = delta_zero + back_product(first_layer_taps[1], full_one[1])
    delta_zero = delta_zero + back_product(first_layer_taps[2], full_one[2])
    input_grad = (middle_gradient.astype(jnp.float32) + gelu_slope(inputs_f) * delta_zero).astype(
        jnp.bfloat16
    )
    part_one = jnp.stack(
        [outer_terms(input_activation, first_layer_taps[k], factor) for k in range(3)]
    ).astype(jnp.bfloat16)
    grad_one = lax.psum(
        lax.psum_scatter(part_one, "dp", scatter_dimension=2, tiled=True).astype(jnp.float32), "seq"
    )
    return (input_grad.reshape(inputs.shape), grad_one, grad_two)


def on_device(inputs, *others):
    seq, dp = lax.axis_size("seq"), lax.axis_size("dp")
    if (
        seq == 2 * FIRST_SHIFT
        and seq <= SECOND_SHIFT
        and dp == 4
        and inputs.shape[0] == 1
        and inputs.shape[1] % (256 * CHUNKS) == 0
    ):
        return on_pairs(inputs, *others)
    return on_shifts(inputs, *others)


def solution(mesh):
    placed = (
        P(("groups", "dp"), "seq", None),
        P(("groups", "dp"), "seq", None),
        P(None, None, "dp"),
        P(None, None, "dp"),
    )
    return jax.shard_map(
        on_device,
        mesh=mesh,
        in_specs=placed,
        out_specs=(
            P(("groups", "dp"), "seq", None),
            P("groups", None, "dp"),
            P("groups", None, "dp"),
        ),
        check_vma=False,
    )
```

```python
import functools
import math

import jax
import jax.numpy as jnp
from jax import lax
from jax.experimental import pallas as pl
from jax.experimental.pallas import tpu as pltpu
from jax.sharding import PartitionSpec as P

FIRST_SHIFT = 2
SECOND_SHIFT = 4
CHUNKS = 2
F32 = jnp.float32
BF16 = jnp.bfloat16


def gelu_pair(x):
    s = math.sqrt(2.0 / math.pi)
    square = x * x
    half = 0.5 + 0.5 * jnp.tanh(x * (s + (0.044715 * s) * square))
    bend = x * (2.0 * s + (6.0 * 0.044715 * s) * square)
    return x * half, half * (1.0 + (1.0 - half) * bend)


def dot_nn(a, b):
    return lax.dot_general(a, b, (((1,), (0,)), ((), ())), preferred_element_type=F32)


def dot_nt(a, b):
    return lax.dot_general(a, b, (((1,), (1,)), ((), ())), preferred_element_type=F32)


def dot_tn(a, b):
    return lax.dot_general(a, b, (((0,), (0,)), ((), ())), preferred_element_type=F32)


VMEM = pl.BlockSpec(memory_space=pltpu.VMEM)
SMEM = pl.BlockSpec(memory_space=pltpu.SMEM)
ANY = pl.BlockSpec(memory_space=pl.ANY)
HBM = pl.BlockSpec(memory_space=pltpu.HBM)


def call(body, name, out, operands, specs, out_specs=None, scratch=(), aliases=None, limit=8):
    return pl.pallas_call(
        body,
        out_shape=[jax.ShapeDtypeStruct(*o) for o in out],
        in_specs=specs,
        out_specs=out_specs or [VMEM] * len(out),
        scratch_shapes=scratch,
        input_output_aliases=aliases or {},
        compiler_params=pltpu.CompilerParams(vmem_limit_bytes=limit << 20),
        name=name,
    )(*operands)


def lanes(start, size):
    return pl.ds(pl.multiple_of(start, 128), size)


def pack_kernel(start, where, x_ref, c_ref, *refs):
    wire_ref, sems = refs[-2:]
    at = lanes(where[4] + start, wire_ref.shape[2])
    copies = [
        pltpu.make_async_copy(ref.at[:, at], wire_ref.at[j], sems.at[j])
        for j, ref in enumerate((x_ref, c_ref))
    ]
    for copy in copies:
        copy.start()
    for copy in copies:
        copy.wait()


def turn_kernel(w_ref, w2_ref, after_ref, out_ref, taps, sems):
    del after_ref
    copies = [
        pltpu.make_async_copy(w_ref, taps.at[pl.ds(0, 3)], sems.at[0]),
        pltpu.make_async_copy(w2_ref.at[1], taps.at[3], sems.at[1]),
    ]
    for copy in copies:
        copy.start()
    for copy in copies:
        copy.wait()
    for k in range(4):
        out_ref[k] = taps[k].T


def join_kernel(where, *refs):
    pieces, (out_ref, across_ref) = refs[:-2], refs[-2:]
    shard = pieces[0].shape[1]
    for m, ref in enumerate(pieces):
        rows = pl.ds(pl.multiple_of(lax.bitwise_xor(where[3], m) * shard, 16), shard)
        for k in range(4):
            out_ref[k, rows, :] = ref[k]
    for k in range(4):
        across_ref[k] = out_ref[k].T


def both(o_ref, where, start, size, wire):
    return jnp.concatenate([o_ref[:, lanes(where[0] + start, size)], wire], axis=1)


def own_part(where, start, size, x_ref, c_ref, w_ref, across_ref, outs):
    act_ref, base_ref, cross_ref, delta_ref = outs
    at = lanes(where[0] + start, size)
    x = x_ref[:, at].astype(F32)
    act = gelu_pair(x)[0].astype(BF16)
    act_ref[...] = act
    base_ref[...] = x + dot_nn(w_ref[1], act)
    cross_ref[...] = dot_nn(w_ref[2 - where[1]], act)
    delta_ref[...] = dot_nn(across_ref[3], c_ref[:, at])


def weight_terms(q, cot, act, act_one, mid, size):
    act_o, act_p = act[:, :size], act[:, size:]
    mid_o, mid_p = mid[:, :size], mid[:, size:]
    return ((3, cot, act_one), (1, mid, act), (q, mid_o, act_p), (2 - q, mid_p, act_o))


def first_kernel(later, where, x_ref, c_ref, wire_ref, w_ref, across_ref, mid_ref, sums, *outs):
    size = wire_ref.shape[2]
    q = where[1]
    x = both(x_ref, where, 0, size, wire_ref[0]).astype(F32)
    cot = both(c_ref, where, 0, size, wire_ref[1])
    act = gelu_pair(x)[0].astype(BF16)
    act_o, act_p = act[:, :size], act[:, size:]
    cross = jnp.concatenate([dot_nn(w_ref[q], act_p), dot_nn(w_ref[2 - q], act_o)], axis=1)
    hidden = (x + dot_nn(w_ref[1], act) + cross).astype(BF16).astype(F32)
    act_one, slope_one = gelu_pair(hidden)
    mid = (cot.astype(F32) + slope_one * dot_nn(across_ref[3], cot)).astype(BF16)
    mid_ref[...] = mid
    for k, left, right in weight_terms(q, cot, act, act_one.astype(BF16), mid, size):
        sums[k] = dot_nt(left, right)
    own_part(where, size, later, x_ref, c_ref, w_ref, across_ref, outs)


def row_parts(shard):
    main = shard // 32 * 16
    rest = shard // 2 - main
    return (
        (slice(0, main), slice(2 * main, 2 * main + rest)),
        (slice(main, 2 * main), slice(2 * main + rest, shard)),
    )


def last_kernel(start, factor, where, c_ref, wire_ref, w_ref, across_ref, sums, *refs):
    act_ref, base_ref, cross_ref, delta_ref, mid_ref = refs[:5]
    outs, total = refs[5:-1], refs[-1]
    size = wire_ref.shape[2]
    q = where[1]
    x_p = wire_ref[0].astype(F32)
    cot_p = wire_ref[1]
    act_p = gelu_pair(x_p)[0].astype(BF16)
    hidden = jnp.concatenate(
        [
            base_ref[...] + dot_nn(w_ref[q], act_p),
            x_p + dot_nn(w_ref[1], act_p) + cross_ref[...],
        ],
        axis=1,
    )
    act_one, slope_one = gelu_pair(hidden.astype(BF16).astype(F32))
    cot = both(c_ref, where, start, size, cot_p)
    delta = jnp.concatenate([delta_ref[...], dot_nn(across_ref[3], cot_p)], axis=1)
    mid = (cot.astype(F32) + slope_one * delta).astype(BF16)
    mid_ref[...] = mid
    act = jnp.concatenate([act_ref[...], act_p], axis=1)
    for k, left, right in weight_terms(q, cot, act, act_one.astype(BF16), mid, size):
        total[k] = ((sums[k] + dot_nt(left, right)) * factor).astype(BF16)
    shard = 2 * outs[0].shape[2]
    for given in range(2):
        core = lax.bitwise_xor(where[2], given)
        for j in range(2):
            side = lax.bitwise_xor(where[6], 1 - j)
            rows = pl.ds(pl.multiple_of((2 * side + core) * shard, 16), shard)
            for k in range(2):
                level = lax.bitwise_xor(where[5], 1 - k)
                pair = [total[level, rows, :], total[level + 2, rows, :]]
                pair = jnp.concatenate(pair, axis=1)
                for h, (main, rest) in enumerate(row_parts(shard)):
                    out = outs[2 * h + given]
                    out[j, k, : main.stop - main.start] = pair[main]
                    out[j, k, main.stop - main.start :] = pair[rest]


def back_kernel(start, where, x_ref, wire_ref, mid_ref, across_ref, own_ref, give_ref):
    size = wire_ref.shape[2]
    q = where[1]
    r = 2 - q
    slope = gelu_pair(both(x_ref, where, start, size, wire_ref[0]).astype(F32))[1]
    mid = mid_ref[...]
    mid_o, mid_p = mid[:, :size], mid[:, size:]
    cross = jnp.concatenate([dot_nn(across_ref[r], mid_p), dot_nn(across_ref[q], mid_o)], axis=1)
    delta = dot_nn(across_ref[1], mid) + cross
    grad = (mid.astype(F32) + slope * delta).astype(BF16)
    own_ref[...] = grad[:, :size]
    give_ref[...] = grad[:, size:]


def finish_kernel(other, where, *refs):
    (one_ref, two_ref), (turned, zeros, sems) = refs[-5:-3], refs[-3:]
    terms = refs[: len(refs) - 5 - (2 if other else 0)]
    chans = turned.shape[1]
    if not other:
        zeros[...] = jnp.zeros(zeros.shape, F32)
        blank = [pltpu.make_async_copy(zeros, two_ref.at[k], sems.at[2 + k]) for k in (0, 2)]
        for copy in blank:
            copy.start()
    halves = [ref[...].astype(F32) for ref in terms]
    main = turned.shape[2] // 32 * 16
    rows = jnp.concatenate([v[:main] for v in halves] + [v[main:] for v in halves], axis=0)
    for j in range(2):
        turned[j] = rows[:, j * chans : (j + 1) * chans].T
    parity = lax.bitwise_xor(where[5], 1) if other else where[5]
    for want, places in ((0, ((one_ref, 0), (one_ref, 2))), (1, ((one_ref, 1), (two_ref, 1)))):

        @pl.when(parity == want)
        def _():
            copies = [
                pltpu.make_async_copy(turned.at[j], ref.at[k], sems.at[j])
                for j, (ref, k) in enumerate(places)
            ]
            for copy in copies:
                copy.start()
            for copy in copies:
                copy.wait()

    if not other:
        for copy in blank:
            copy.wait()


def finished(where, terms, chans, shard, held=()):
    return call(
        functools.partial(finish_kernel, bool(held)),
        "finish",
        [((3, chans, shard), F32)] * 2,
        [where, *terms, *held],
        [SMEM] + [VMEM] * len(terms) + [HBM] * len(held),
        out_specs=[HBM, HBM],
        scratch=[
            pltpu.VMEM((2, chans, shard), F32),
            pltpu.VMEM((chans, shard), F32),
            pltpu.SemaphoreType.DMA((5,)),
        ],
        aliases={len(terms) + 1 + j: j for j in range(len(held))},
    )


def place_kernel(plan, where, *refs):
    pieces, (out_ref, sems) = refs[: len(plan)], refs[-2:]
    copies = [
        pltpu.make_async_copy(
            ref,
            out_ref.at[pl.ds(row, ref.shape[0]), lanes(where[base] + start, ref.shape[1])],
            sems.at[i],
        )
        for i, (ref, (base, row, start)) in enumerate(zip(pieces, plan))
    ]
    for copy in copies:
        copy.start()
    for copy in copies:
        copy.wait()


def placed(where, plan, pieces, shape, after):
    (out,) = call(
        functools.partial(place_kernel, plan),
        "place",
        [(shape, BF16)],
        [where, *pieces, after],
        [SMEM] + [VMEM] * len(pieces) + [ANY],
        out_specs=[HBM],
        scratch=[pltpu.SemaphoreType.DMA((len(pieces),))],
    )
    return out


def in_hbm(value):
    return pltpu.with_memory_space_constraint(value, pltpu.HBM)


def swapped(value, axis, bit):
    route = [(i, i ^ bit) for i in range(lax.axis_size(axis))]
    return lax.ppermute(value, axis, route)


def added(a, b):
    return (a.astype(F32) + b.astype(F32)).astype(BF16)


def on_pairs(inputs, cotangent, first_weight_matrix, weight_two):
    chans = inputs.shape[2]
    block = inputs.shape[1]
    shard = chans // 4
    half = block // 2
    sizes = [half // CHUNKS] * CHUNKS
    factor = 1.0 / math.sqrt(
        inputs.shape[0] * lax.axis_size("dp") * inputs.shape[1] * lax.axis_size("seq")
    )
    seq, dp = lax.axis_index("seq"), lax.axis_index("dp")
    low = seq < FIRST_SHIFT
    keep_at = jnp.where(low, 0, half)
    level, side, core = seq % 2, dp // 2, dp % 2
    where = jnp.stack([keep_at, jnp.where(low, 2, 0), core, dp, half - keep_at, level, side])
    where = where.astype(jnp.int32)
    x, cot = inputs.reshape(block, chans).T, cotangent.reshape(block, chans).T

    packed, start = [], 0
    for size in sizes:
        packed += call(
            functools.partial(pack_kernel, start),
            "pack",
            [((2, chans, size), BF16)],
            [where, in_hbm(x), in_hbm(cot)] + packed[-1:],
            [SMEM, HBM, HBM] + [ANY] * len(packed[-1:]),
            scratch=[pltpu.SemaphoreType.DMA((2,))],
        )
        start += size
    wires = [swapped(wire, "seq", FIRST_SHIFT) for wire in packed]
    (own_shard,) = call(
        turn_kernel,
        "turn",
        [((4, shard, chans), BF16)],
        [in_hbm(first_weight_matrix), in_hbm(weight_two), packed[-1]],
        [HBM, HBM, ANY],
        scratch=[pltpu.VMEM((4, chans, shard), BF16), pltpu.SemaphoreType.DMA((2,))],
    )
    shards = [own_shard] + [swapped(own_shard, "dp", m) for m in (1, 2, 3)]
    w, across = call(
        join_kernel,
        "join",
        [((4, chans, chans), BF16)] * 2,
        [where, *shards],
        [SMEM] + [VMEM] * 4,
    )

    def backward(c, mid):
        return call(
            functools.partial(back_kernel, c * size),
            f"back_{c}",
            [((chans, size), BF16)] * 2,
            [where, x, wires[c], mid, across],
            [SMEM] + [VMEM] * 4,
        )

    size = half // CHUNKS
    own = []
    mid, *held = call(
        functools.partial(first_kernel, size),
        "first",
        [((chans, 2 * size), BF16), ((4, chans, chans), F32), ((chans, size), BF16)]
        + [((chans, size), F32)] * 3,
        [where, x, cot, wires[0], w, across],
        [SMEM] + [VMEM] * 5,
    )
    mine, theirs = backward(0, mid)
    own.append(mine)
    back = [theirs]
    back[0], wires[1] = lax.optimization_barrier((back[0], wires[1]))
    mid, *halves = call(
        functools.partial(last_kernel, size, factor),
        "last",
        [((chans, 2 * size), BF16)]
        + [((2, 2, shard // 2, 2 * chans), BF16)] * 4,
        [where, cot, wires[1], w, across, *held],
        [SMEM] + [VMEM] * 9,
        scratch=[pltpu.VMEM((4, chans, chans), BF16)],
    )

    tie = lambda *values: list(lax.optimization_barrier(values))
    keep, give = halves[0::2], halves[1::2]
    returned = [swapped(back[0], "seq", FIRST_SHIFT)]
    got = [swapped(v, "dp", 1) for v in give]
    send = [added(k[0], v[0]) for k, v in zip(keep, got)]
    mine = [added(k[1], v[1]) for k, v in zip(keep, got)]
    send[0], mid = tie(send[0], mid)
    own_last, theirs = backward(1, mid)
    own.append(own_last)
    cut = chans // 2
    first, second = theirs[:cut], theirs[cut:]
    send = tie(*send)
    got = [swapped(v, "dp", 2) for v in send]
    got[1], first = tie(got[1], first)
    returned.append(swapped(first, "seq", FIRST_SHIFT))
    send = [added(m[0], v[0]) for m, v in zip(mine, got)]
    mine = [added(m[1], v[1]) for m, v in zip(mine, got)]
    send[0], mine[1] = tie(send[0], mine[1])
    got = [swapped(v, "seq", 1) for v in send]
    got[0], second = tie(got[0], second)
    returned.append(swapped(second, "seq", FIRST_SHIFT))
    mine = [added(m, v) for m, v in zip(mine, got)]
    mine = [added(m, swapped(m, "seq", 2)) for m in mine]
    theirs = [swapped(m, "seq", 1) for m in mine]
    input_grad = placed(
        where,
        ((0, 0, 0), (0, 0, size), (4, 0, 0), (4, 0, size), (4, cut, size)),
        own + returned,
        (chans, block),
        mine[0],
    )
    held = finished(where, mine, chans, shard)
    grad_one, grad_two = finished(where, theirs, chans, shard, held)
    return (input_grad.T.reshape(inputs.shape), grad_one, grad_two)


def shifted(block, axis, distance):
    devices = range(lax.axis_size(axis))
    route = [(i - distance, i) for i in devices if i - distance in devices]
    return lax.ppermute(block, axis, route)


def gelu_slope(value):
    return jax.vjp(jax.nn.gelu, value)[1](jnp.ones_like(value))[0]


def outer_terms(left, right, factor):
    product = lax.dot_general(
        left, right, (((0,), (0,)), ((), ())), preferred_element_type=jnp.float32
    )
    return product * factor


def back_product(tap, weight):
    return lax.dot_general(
        tap, weight, (((1,), (1,)), ((), ())), preferred_element_type=jnp.float32
    )


def on_shifts(inputs, cotangent, first_weight_matrix, weight_two):
    chans = inputs.shape[2]
    rows = inputs.shape[0] * inputs.shape[1]
    factor = 1.0 / math.sqrt(
        inputs.shape[0] * lax.axis_size("dp") * inputs.shape[1] * lax.axis_size("seq")
    )
    full_one = lax.all_gather(first_weight_matrix, "dp", axis=2, tiled=True)
    flat_in = inputs.reshape(rows, chans)
    inputs_f = flat_in.astype(jnp.float32)
    input_activation = jax.nn.gelu(inputs_f).astype(jnp.bfloat16)
    act_before = shifted(input_activation, "seq", 2)
    act_after = shifted(input_activation, "seq", -2)
    flat_cot = cotangent.reshape(rows, chans)
    cot_later = shifted(flat_cot, "seq", -4)
    cot_earlier = shifted(flat_cot, "seq", 4)
    preactivation = jnp.dot(act_before, full_one[0], preferred_element_type=jnp.float32)
    preactivation = preactivation + jnp.dot(
        input_activation, full_one[1], preferred_element_type=jnp.float32
    )
    preactivation = preactivation + jnp.dot(
        act_after, full_one[2], preferred_element_type=jnp.float32
    )
    hidden_f = (inputs_f + preactivation).astype(jnp.bfloat16).astype(jnp.float32)
    act_one = jax.nn.gelu(hidden_f).astype(jnp.bfloat16)
    full_two = lax.all_gather(weight_two, "dp", axis=2, tiled=True)
    second_layer_taps = (cot_later, flat_cot, cot_earlier)
    delta_one = back_product(second_layer_taps[0], full_two[0])
    delta_one = delta_one + back_product(second_layer_taps[1], full_two[1])
    delta_one = delta_one + back_product(second_layer_taps[2], full_two[2])
    middle_gradient = (flat_cot.astype(jnp.float32) + gelu_slope(hidden_f) * delta_one).astype(
        jnp.bfloat16
    )
    part_two = jnp.stack(
        [outer_terms(act_one, second_layer_taps[k], factor) for k in range(3)]
    ).astype(jnp.bfloat16)
    grad_two = lax.psum(
        lax.psum_scatter(part_two, "dp", scatter_dimension=2, tiled=True).astype(jnp.float32), "seq"
    )
    grad_later = shifted(middle_gradient, "seq", -2)
    grad_earlier = shifted(middle_gradient, "seq", 2)
    first_layer_taps = (grad_later, middle_gradient, grad_earlier)
    delta_zero = back_product(first_layer_taps[0], full_one[0])
    delta_zero = delta_zero + back_product(first_layer_taps[1], full_one[1])
    delta_zero = delta_zero + back_product(first_layer_taps[2], full_one[2])
    input_grad = (middle_gradient.astype(jnp.float32) + gelu_slope(inputs_f) * delta_zero).astype(
        jnp.bfloat16
    )
    part_one = jnp.stack(
        [outer_terms(input_activation, first_layer_taps[k], factor) for k in range(3)]
    ).astype(jnp.bfloat16)
    grad_one = lax.psum(
        lax.psum_scatter(part_one, "dp", scatter_dimension=2, tiled=True).astype(jnp.float32), "seq"
    )
    return (input_grad.reshape(inputs.shape), grad_one, grad_two)


def on_device(inputs, *others):
    seq, dp = lax.axis_size("seq"), lax.axis_size("dp")
    if (
        seq == 2 * FIRST_SHIFT
        and seq <= SECOND_SHIFT
        and dp == 4
        and inputs.shape[0] == 1
        and inputs.shape[1] % (256 * CHUNKS) == 0
    ):
        return on_pairs(inputs, *others)
    return on_shifts(inputs, *others)


def solution(mesh):
    placed = (
        P(("groups", "dp"), "seq", None),
        P(("groups", "dp"), "seq", None),
        P(None, None, "dp"),
        P(None, None, "dp"),
    )
    return jax.shard_map(
        on_device,
        mesh=mesh,
        in_specs=placed,
        out_specs=(
            P(("groups", "dp"), "seq", None),
            P("groups", None, "dp"),
            P("groups", None, "dp"),
        ),
        check_vma=False,
    )
```
